32 devices in a mesh: dp: 16 (over z, x, core), tensor: 2 (over y).
Axes of the slice: x: 2, y: 2, z: 4, core: 2. Of those that a mesh axis runs over, the one named last changes fastest.
Arguments:
- hidden_in: bfloat16 [16384, 1024], P(('dp', 'tensor')), may hold values from -6 to 6
- out_cotangent: bfloat16 [16384, 1024], P(('dp', 'tensor')), may hold values from -6 to 6
- segment_ids: int32 [16, 1024], P('dp'), may hold values from 0 to 2, never falling along the last dimension, each value on 1 to 512 neighbouring positions
- joined_weight: float32 [1024, 3072], P('dp', 'tensor'), may hold values from -0.1875 to 0.1875
- dense_weight: float32 [1024, 1024], P('tensor', 'dp'), may hold values from -0.375 to 0.375
- upward_weight: float32 [1024, 4096], P('dp', 'tensor'), may hold values from -0.1875 to 0.1875
- downward_weight: float32 [4096, 1024], P('tensor', 'dp'), may hold values from -0.09375 to 0.09375
- head_bias: float32 [2, 1024], P(None, 'tensor'), may hold values from -3 to 3
- upward_bias: float32 [4096], P('tensor'), may hold values from -3 to 3
- norm_gain: float32 [2, 1024], replicated, may hold values from 0.5 to 1.5
- row_bias: float32 [4, 1024], replicated, may hold values from -1.75 to 1.75
- joined_momentum: float32 [1024, 3072], P('dp', 'tensor'), may hold values from -80 to 80
- dense_momentum: float32 [1024, 1024], P('tensor', 'dp'), may hold values from -80 to 80
- upward_momentum: float32 [1024, 4096], P('dp', 'tensor'), may hold values from -80 to 80
- downward_momentum: float32 [4096, 1024], P('tensor', 'dp'), may hold values from -80 to 80
- head_bias_momentum: float32 [2, 1024], P(None, 'tensor'), may hold values from -80 to 80
- upward_bias_momentum: float32 [4096], P('tensor'), may hold values from -80 to 80
- norm_gain_momentum: float32 [2, 1024], replicated, may hold values from -80 to 80
- row_bias_momentum: float32 [4, 1024], replicated, may hold values from -80 to 80
Outputs:
- block_out: bfloat16 [16384, 1024], P(('dp', 'tensor'))
- input_grad: float32 [16384, 1024], P(('dp', 'tensor'))
- joined_grad: float32 [1024, 3072], P('dp', 'tensor')
- dense_grad: float32 [1024, 1024], P('tensor', 'dp')
- upward_grad: float32 [1024, 4096], P('dp', 'tensor')
- downward_grad: float32 [4096, 1024], P('tensor', 'dp')
- head_bias_grad: float32 [2, 1024], P(None, 'tensor')
- upward_bias_grad: float32 [4096], P('tensor')
- norm_gain_grad: float32 [2, 1024], replicated
- row_bias_grad: float32 [4, 1024], replicated
- joined_weight_new: float32 [1024, 3072], P('dp', 'tensor')
- dense_weight_new: float32 [1024, 1024], P('tensor', 'dp')
- upward_weight_new: float32 [1024, 4096], P('dp', 'tensor')
- downward_weight_new: float32 [4096, 1024], P('tensor', 'dp')
- head_bias_new: float32 [2, 1024], P(None, 'tensor')
- upward_bias_new: float32 [4096], P('tensor')
- norm_gain_new: float32 [2, 1024], replicated
- row_bias_new: float32 [4, 1024], replicated
- joined_momentum_new: float32 [1024, 3072], P('dp', 'tensor')
- dense_momentum_new: float32 [1024, 1024], P('tensor', 'dp')
- upward_momentum_new: float32 [1024, 4096], P('dp', 'tensor')
- downward_momentum_new: float32 [4096, 1024], P('tensor', 'dp')
- head_bias_momentum_new: float32 [2, 1024], P(None, 'tensor')
- upward_bias_momentum_new: float32 [4096], P('tensor')
- norm_gain_momentum_new: float32 [2, 1024], replicated
- row_bias_momentum_new: float32 [4, 1024], replicated
The draws below stay inside these ranges and needn't reach their ends.
Inputs may be any that keep to these rules, and one draw needn't show every extreme that they name: `segment_ids`: segment numbers never fall along a sequence; each document holds at most 512 tokens, and some document holds exactly 512.
All inputs are finite; a program needn't handle non-finite values.
Results may differ from the reference program's by a relative error of at most 0.018.
Values may be sent and summed in bfloat16 or wider, within the bound.
A program may use at most 192 MiB of HBM per device.

```python
import math
import jax
import jax.numpy as jnp
import numpy as np
from jax import lax

D = 1024
H = 16
HD = 64
FF = 4096
LENGTH = 1024
DOCS = 3
MB = 256
NS_STEPS = 5
DOC_MAX = 512
GROUPS = 2
SEQS = 16
TOKENS = 16384


def with_spikes(entries, rng, source, target, shards_of, factor):
    owner, partner = [(jnp.arange(entries.shape[axis_at]) // (entries.shape[axis_at] // shards_of)).reshape([-1 if axis == axis_at else 1 for axis in range(entries.ndim)]) for axis_at in (source, target)]
    chosen = jax.random.permutation(rng, shards_of)[partner]
    strong = (owner == chosen) | (owner == (partner + shards_of // 2) % shards_of)
    return jnp.where(strong, factor * entries, entries)


def level_of(stream_key, shape, pieces, smallest, high):
    def one(dim, parts):
        steps = jax.random.uniform(jax.random.fold_in(jax.random.fold_in(stream_key, 6), dim), (parts,), jnp.float32, smallest / len(pieces), high / len(pieces))
        return jnp.repeat(jnp.exp(steps), shape[dim] // parts).reshape((-1,) + (1,) * (len(shape) - dim - 1))

    level = one(*pieces[0])
    for cut in pieces[1:]:
        level = level * one(*cut)
    return level


def length_profile(count, total, most, slope):
    loads = [(1 << 20) // math.isqrt(grade ** slope) + 1 for grade in range(2, count + 1)]
    surplus, holding = total - most - (count - 1), [1] * (count - 1)
    while surplus > 0:
        candidates = [i for i in range(count - 1) if holding[i] < most]
        whole, left = sum([loads[i] for i in candidates]), surplus
        for i in candidates:
            more = min(most - holding[i], max(1, left * loads[i] // whole), surplus)
            holding[i] = holding[i] + more
            surplus = surplus - more
    return np.array([most] + holding)


def uneven_parts(stream_key, count, total, most, slope):
    if count == 2:
        one = jax.random.randint(stream_key, (), max(1, total - most), min(most, total - 1) + 1)
        return jnp.stack([one, total - one])
    tallies = jnp.asarray(length_profile(count, total, most, slope), jnp.int32)
    couples = (count - 1) // 2
    donor, taker = tallies[1:1 + 2 * couples:2], tallies[2:2 + 2 * couples:2]
    margin = jnp.minimum(donor - 1, most - taker)
    moved = jax.random.randint(jax.random.fold_in(stream_key, 1), (couples,), 0, 1 << 20) % (margin + 1)
    tallies = tallies.at[1:1 + 2 * couples:2].set(donor - moved).at[2:2 + 2 * couples:2].set(taker + moved)
    return tallies[jax.random.permutation(jax.random.fold_in(stream_key, 2), count)]


def scatter_about(own_key, shape, scale, most, cuts=(), kind=jnp.bfloat16):
    gain = level_of(own_key, shape, cuts, -0.22, 0.18) if cuts else 1.0
    values = jax.random.normal(own_key, shape, jnp.float32) * scale * gain
    return jnp.minimum(jnp.maximum(values, -most), most).astype(kind)


def heavy_noise(key, shape, spread, reach, pieces, heavy, kind=jnp.bfloat16):
    entries = spread * jax.random.normal(key, shape, jnp.float32)
    if pieces:
        entries = entries * level_of(key, shape, pieces, -0.22, 0.18)
    return jnp.clip(with_spikes(entries, jax.random.fold_in(key, 3), *heavy), -reach, reach).astype(kind)


def setup_inputs(seed: int = 0) -> dict:
    seeds = jax.random.split(jax.random.key(seed), 20)
    return {
        "hidden_in": heavy_noise(seeds[0], (TOKENS, D), 1.0, 6.0, ((0, 32),), (0, 1, 32, 2.75)),
        "out_cotangent": heavy_noise(seeds[1], (TOKENS, D), 1.0, 6.0, ((0, 32),), (0, 1, 32, 2.75)),
        "segment_ids": jax.vmap(lambda own: jnp.searchsorted(jnp.cumsum(uneven_parts(own, DOCS, LENGTH, DOC_MAX, 1)), jnp.arange(LENGTH), side="right"))(jax.random.split(seeds[2], SEQS)).reshape((SEQS, LENGTH)).astype(jnp.int32),
        "joined_weight": scatter_about(seeds[3], (D, 3 * D), D ** -0.5, 0.1875, ((0, 16), (1, 2)), jnp.float32),
        "dense_weight": scatter_about(seeds[4], (D, D), (D // 4) ** -0.5, 0.375, ((0, 2), (1, 16)), jnp.float32),
        "upward_weight": scatter_about(seeds[5], (D, FF), D ** -0.5, 0.1875, ((0, 16), (1, 2)), jnp.float32),
        "downward_weight": scatter_about(seeds[6], (FF, D), FF ** -0.5, 0.09375, ((0, 2), (1, 16)), jnp.float32),
        "head_bias": scatter_about(seeds[7], (2, D), 0.5, 3.0, ((1, 2),), jnp.float32),
        "upward_bias": scatter_about(seeds[8], (FF,), 0.5, 3.0, ((0, 2),), jnp.float32),
        "norm_gain": jnp.clip(1.0 + 0.1 * jax.random.normal(seeds[9], (2, D), jnp.float32), 0.5, 1.5),
        "row_bias": scatter_about(seeds[10], (4, D), 0.3, 1.75, (), jnp.float32),
        "joined_momentum": scatter_about(seeds[11], (D, 3 * D), (0.1 * TOKENS ** 0.5), 80.0, ((0, 16), (1, 2)), jnp.float32),
        "dense_momentum": scatter_about(seeds[12], (D, D), (0.1 * TOKENS ** 0.5), 80.0, ((0, 2), (1, 16)), jnp.float32),
        "upward_momentum": scatter_about(seeds[13], (D, FF), (0.1 * TOKENS ** 0.5), 80.0, ((0, 16), (1, 2)), jnp.float32),
        "downward_momentum": scatter_about(seeds[14], (FF, D), (0.1 * TOKENS ** 0.5), 80.0, ((0, 2), (1, 16)), jnp.float32),
        "head_bias_momentum": scatter_about(seeds[15], (2, D), (0.1 * TOKENS ** 0.5), 80.0, ((1, 2),), jnp.float32),
        "upward_bias_momentum": scatter_about(seeds[16], (FF,), (0.1 * TOKENS ** 0.5), 80.0, ((0, 2),), jnp.float32),
        "norm_gain_momentum": scatter_about(seeds[17], (2, D), (0.1 * TOKENS ** 0.5), 80.0, (), jnp.float32),
        "row_bias_momentum": scatter_about(seeds[18], (4, D), (0.1 * TOKENS ** 0.5), 80.0, (), jnp.float32),
    }


MOMENTUM_BETA = 0.95
MUON_RATE = 0.04
VECTOR_RATE = 0.1
NORM_EPSILON = 1e-05
SCHULZ_FIRST = 3.4445
SCHULZ_SECOND = -4.775
SCHULZ_THIRD = 2.0315
GELU_COEFF = 0.7978845608
GELU_CUBIC = 0.044715

def gelu_value(preact):
    inner_arg = GELU_COEFF * (preact + GELU_CUBIC * preact * preact * preact)
    return 0.5 * preact * (1.0 + jnp.tanh(inner_arg))

def gelu_slope(preact):
    tangent = jnp.tanh(GELU_COEFF * (preact + GELU_CUBIC * preact * preact * preact))
    return 0.5 * (1.0 + tangent) + 0.5 * preact * (1.0 - tangent * tangent) * GELU_COEFF * (1.0 + 3.0 * GELU_CUBIC * preact * preact)

def layer_norm(values, gain_row, shift_row):
    average = lax.optimization_barrier(jnp.mean(values, axis=-1, keepdims=True))
    centered = values - average
    variance = lax.optimization_barrier(jnp.mean(centered * centered, axis=-1, keepdims=True))
    inv_std = lax.rsqrt(variance + NORM_EPSILON)
    normed = centered * inv_std
    return (normed * gain_row + shift_row, normed, inv_std)

def norm_backward(upstream, normed, inv_std, gain_row):
    scaled = upstream * gain_row
    inner_mean = lax.optimization_barrier(jnp.mean(scaled, axis=-1, keepdims=True))
    cross_mean = lax.optimization_barrier(jnp.mean(scaled * normed, axis=-1, keepdims=True))
    return (inv_std * (scaled - inner_mean - normed * cross_mean), lax.optimization_barrier(jnp.sum(upstream * normed, axis=0)), lax.optimization_barrier(jnp.sum(upstream, axis=0)))

def newton_schulz(matrix):
    frobenius = jnp.sqrt(jnp.sum(matrix * matrix))
    iterate = (matrix / (frobenius + 1e-07)).astype(jnp.bfloat16)
    for step_number in range(NS_STEPS):
        gram_matrix = jnp.dot(iterate.T, iterate, preferred_element_type=jnp.float32).astype(jnp.bfloat16)
        square = jnp.dot(gram_matrix, gram_matrix, preferred_element_type=jnp.float32)
        polynomial = (SCHULZ_SECOND * gram_matrix.astype(jnp.float32) + SCHULZ_THIRD * square).astype(jnp.bfloat16)
        iterate = (SCHULZ_FIRST * iterate.astype(jnp.float32) + jnp.dot(iterate, polynomial, preferred_element_type=jnp.float32)).astype(jnp.bfloat16)
    return iterate

def vector_step(weight, momentum, gradient):
    new_momentum = MOMENTUM_BETA * momentum + gradient
    blocks = new_momentum.reshape(-1, HD)
    scaled = blocks * lax.rsqrt(lax.optimization_barrier(jnp.mean(blocks * blocks, axis=-1, keepdims=True)) + 1e-06)
    return (weight - VECTOR_RATE * scaled.reshape(weight.shape), new_momentum)

def attention_pieces(joined_part, dense_part, head_count):
    row_total = joined_part.shape[0]
    joined_units = joined_part.reshape(row_total, head_count, 3, HD).transpose(1, 2, 0, 3).reshape(3 * head_count, row_total, HD)
    dense_units = dense_part.reshape(head_count, HD, row_total).transpose(0, 2, 1)
    return jnp.concatenate([joined_units, dense_units], axis=0)

def attention_restore(unit_stack, head_count):
    row_total = unit_stack.shape[1]
    joined_part = unit_stack[:3 * head_count].reshape(head_count, 3, row_total, HD).transpose(2, 0, 1, 3).reshape(row_total, 3 * head_count * HD)
    dense_part = unit_stack[3 * head_count:].transpose(0, 2, 1).reshape(head_count * HD, row_total)
    return (joined_part, dense_part)

def feed_pieces(upward, downward):
    row_total = upward.shape[0]
    block_count = upward.shape[1] // MB
    upward_units = upward.reshape(row_total, block_count, MB).transpose(1, 0, 2)
    downward_units = downward.reshape(block_count, MB, row_total).transpose(0, 2, 1)
    return jnp.concatenate([upward_units, downward_units], axis=0)

def feed_restore(unit_stack):
    block_count = unit_stack.shape[0] // 2
    row_total = unit_stack.shape[1]
    upward = unit_stack[:block_count].transpose(1, 0, 2).reshape(row_total, block_count * MB)
    downward = unit_stack[block_count:].transpose(0, 2, 1).reshape(block_count * MB, row_total)
    return (upward, downward)

def group_product(left_side, right_side):
    row_total, inner_total = left_side.shape
    group_width = inner_total // GROUPS
    partials = jnp.einsum('lgk,gkd->gld', left_side.astype(jnp.float32).reshape(row_total, GROUPS, group_width), right_side.astype(jnp.float32).reshape(GROUPS, group_width, right_side.shape[1]), precision=lax.Precision.HIGHEST)
    return lax.optimization_barrier(jnp.sum(partials.astype(jnp.bfloat16).astype(jnp.float32), axis=0))

def reference(hidden_in, out_cotangent, segment_ids, joined_weight, dense_weight, upward_weight, downward_weight, head_bias, upward_bias, norm_gain, row_bias, joined_momentum, dense_momentum, upward_momentum, downward_momentum, head_bias_momentum, upward_bias_momentum, norm_gain_momentum, row_bias_momentum):
    highest = lax.Precision.HIGHEST
    joined_low = joined_weight.astype(jnp.bfloat16)
    dense_low = dense_weight.astype(jnp.bfloat16)
    upward_low = upward_weight.astype(jnp.bfloat16)
    downward_low = downward_weight.astype(jnp.bfloat16)
    slopes = jnp.exp2(-8.0 * (jnp.arange(H) + 1).astype(jnp.float32) / H)
    scale_factor = HD ** (-0.5)

    def one_sequence(totals, packed):
        seq_in, seq_cot, segments = packed
        residual = seq_in.astype(jnp.float32)
        first_out, first_normed, first_inv = layer_norm(residual, norm_gain[0], row_bias[0])
        first_low = first_out.astype(jnp.bfloat16)
        joined_all = jnp.dot(first_low, joined_low, preferred_element_type=jnp.float32).reshape(LENGTH, H, 3, HD)
        queries = (joined_all[:, :, 0] + head_bias[0].reshape(H, HD)).astype(jnp.bfloat16)
        key_vectors = joined_all[:, :, 1].astype(jnp.bfloat16)
        value_vectors = (joined_all[:, :, 2] + head_bias[1].reshape(H, HD)).astype(jnp.bfloat16)
        query_float = queries.astype(jnp.float32)
        key_float = key_vectors.astype(jnp.float32)
        value_float = value_vectors.astype(jnp.float32)
        raw_scores = jnp.einsum('qhd,khd->hqk', query_float, key_float, precision=highest) * scale_factor
        positions = jnp.arange(LENGTH)
        distance = (positions[:, None] - positions[None, :]).astype(jnp.float32)
        allowed = (distance >= 0.0) & (segments[:, None] == segments[None, :])
        scores = jnp.where(allowed[None], raw_scores - slopes[:, None, None] * distance[None], -1e+30)
        log_total = jnp.log(lax.optimization_barrier(jnp.sum(jnp.exp(scores), axis=-1)))
        probabilities = jnp.exp(scores - log_total[:, :, None])
        prob_low = probabilities.astype(jnp.bfloat16)
        attended = jnp.einsum('hqk,khd->qhd', prob_low.astype(jnp.float32), value_float, precision=highest).astype(jnp.bfloat16)
        attended_flat = attended.reshape(LENGTH, D)
        middle = residual + group_product(attended_flat, dense_low) + row_bias[1]
        second_out, second_normed, second_inv = layer_norm(middle, norm_gain[1], row_bias[2])
        second_low = second_out.astype(jnp.bfloat16)
        preact = jnp.dot(second_low, upward_low, preferred_element_type=jnp.float32) + upward_bias
        activation = gelu_value(preact).astype(jnp.bfloat16)
        result = middle + group_product(activation, downward_low) + row_bias[3]
        upstream = seq_cot.astype(jnp.float32)
        downward_part = jnp.dot(activation.T, seq_cot, preferred_element_type=jnp.float32)
        d_preact = jnp.dot(seq_cot, downward_low.T, preferred_element_type=jnp.float32) * gelu_slope(preact)
        d_preact_low = d_preact.astype(jnp.bfloat16)
        upward_part = jnp.dot(second_low.T, d_preact_low, preferred_element_type=jnp.float32)
        d_second = group_product(d_preact_low, upward_low.T)
        d_middle_norm, gain_second, shift_second = norm_backward(d_second, second_normed, second_inv, norm_gain[1])
        d_middle = upstream + d_middle_norm
        d_middle_low = d_middle.astype(jnp.bfloat16)
        dense_part = jnp.dot(attended_flat.T, d_middle_low, preferred_element_type=jnp.float32)
        d_attended = jnp.dot(d_middle_low, dense_low.T, preferred_element_type=jnp.float32).astype(jnp.bfloat16).reshape(LENGTH, H, HD)
        d_attended_float = d_attended.astype(jnp.float32)
        grad_value = jnp.einsum('hqk,qhd->khd', prob_low.astype(jnp.float32), d_attended_float, precision=highest)
        d_probs = jnp.einsum('qhd,khd->hqk', d_attended_float, value_float, precision=highest)
        row_delta = lax.optimization_barrier(jnp.sum(d_attended_float * attended.astype(jnp.float32), axis=-1))
        d_score = (probabilities * (d_probs - row_delta.T[:, :, None])).astype(jnp.bfloat16).astype(jnp.float32)
        grad_query = jnp.einsum('hqk,khd->qhd', d_score, key_float, precision=highest) * scale_factor
        grad_key = jnp.einsum('hqk,qhd->khd', d_score, query_float, precision=highest) * scale_factor
        head_part = jnp.stack([lax.optimization_barrier(jnp.sum(grad_query, axis=0)).reshape(D), lax.optimization_barrier(jnp.sum(grad_value, axis=0)).reshape(D)])
        d_joined = jnp.stack([grad_query, grad_key, grad_value], axis=2).astype(jnp.bfloat16).reshape(LENGTH, 3 * D)
        joined_part = jnp.dot(first_low.T, d_joined, preferred_element_type=jnp.float32)
        d_first = group_product(d_joined, joined_low.T)
        d_input_norm, gain_first, shift_first = norm_backward(d_first, first_normed, first_inv, norm_gain[0])
        input_part = d_middle + d_input_norm
        gain_part = jnp.stack([gain_first, gain_second])
        shift_part = jnp.stack([shift_first, lax.optimization_barrier(jnp.sum(d_middle, axis=0)), shift_second, lax.optimization_barrier(jnp.sum(upstream, axis=0))])
        additions = (joined_part, dense_part, upward_part, downward_part, head_part, lax.optimization_barrier(jnp.sum(d_preact, axis=0)), gain_part, shift_part)
        totals = tuple((older + newer for older, newer in zip(totals, additions)))
        return (totals, (result.astype(jnp.bfloat16), input_part))
    initial = (jnp.zeros((D, 3 * D), jnp.float32), jnp.zeros((D, D), jnp.float32), jnp.zeros((D, FF), jnp.float32), jnp.zeros((FF, D), jnp.float32), jnp.zeros((2, D), jnp.float32), jnp.zeros((FF,), jnp.float32), jnp.zeros((2, D), jnp.float32), jnp.zeros((4, D), jnp.float32))
    totals, (outputs, input_grads) = lax.scan(one_sequence, initial, (hidden_in.reshape(SEQS, LENGTH, D), out_cotangent.reshape(SEQS, LENGTH, D), segment_ids))
    joined_grad, dense_grad, upward_grad, downward_grad, head_bias_grad, upward_bias_grad, norm_gain_grad, row_bias_grad = totals
    block_out = outputs.reshape(TOKENS, D)
    input_grad = input_grads.reshape(TOKENS, D)
    joined_mom_new = MOMENTUM_BETA * joined_momentum + joined_grad
    dense_mom_new = MOMENTUM_BETA * dense_momentum + dense_grad
    upward_mom_new = MOMENTUM_BETA * upward_momentum + upward_grad
    downward_mom_new = MOMENTUM_BETA * downward_momentum + downward_grad
    attn_ortho = lax.map(newton_schulz, attention_pieces(joined_mom_new, dense_mom_new, H)).astype(jnp.float32)
    feed_ortho = lax.map(newton_schulz, feed_pieces(upward_mom_new, downward_mom_new)).astype(jnp.float32)
    joined_ortho, dense_ortho = attention_restore(attn_ortho, H)
    upward_ortho, downward_ortho = feed_restore(feed_ortho)
    muon_step = MUON_RATE * 0.2 * math.sqrt(D)
    joined_new = joined_weight - muon_step * joined_ortho
    dense_new = dense_weight - muon_step * dense_ortho
    upward_new = upward_weight - muon_step * upward_ortho
    downward_new = downward_weight - muon_step * downward_ortho
    head_new, head_mom_new = vector_step(head_bias, head_bias_momentum, head_bias_grad)
    upbias_new, upbias_mom_new = vector_step(upward_bias, upward_bias_momentum, upward_bias_grad)
    gain_new, gain_mom_new = vector_step(norm_gain, norm_gain_momentum, norm_gain_grad)
    shift_new, shift_mom_new = vector_step(row_bias, row_bias_momentum, row_bias_grad)
    return (block_out, input_grad, joined_grad, dense_grad, upward_grad, downward_grad, head_bias_grad, upward_bias_grad, norm_gain_grad, row_bias_grad, joined_new, dense_new, upward_new, downward_new, head_new, upbias_new, gain_new, shift_new, joined_mom_new, dense_mom_new, upward_mom_new, downward_mom_new, head_mom_new, upbias_mom_new, gain_mom_new, shift_mom_new)
```

```python
import functools
import math

import jax
import jax.numpy as jnp
from jax import lax
from jax.experimental import pallas as pl
from jax.experimental.pallas import tpu as pltpu
from jax.sharding import PartitionSpec as P


D = 1024
H = 16
HD = 64
FF = 4096
MB = 256
NS_STEPS = 5


MOMENTUM_BETA = 0.95
MUON_RATE = 0.04
VECTOR_RATE = 0.1
NORM_EPSILON = 1e-05
SCHULZ_FIRST = 3.4445
SCHULZ_SECOND = -4.775
SCHULZ_THIRD = 2.0315
GELU_COEFF = 0.7978845608
GELU_CUBIC = 0.044715


def gelu_value(preact):
    inner_arg = GELU_COEFF * (preact + GELU_CUBIC * preact * preact * preact)
    return 0.5 * preact * (1.0 + jnp.tanh(inner_arg))


def gelu_slope(preact):
    tangent = jnp.tanh(GELU_COEFF * (preact + GELU_CUBIC * preact * preact * preact))
    return 0.5 * (1.0 + tangent) + 0.5 * preact * (1.0 - tangent * tangent) * GELU_COEFF * (
        1.0 + 3.0 * GELU_CUBIC * preact * preact
    )


def layer_norm(values, gain_row, shift_row):
    average = jnp.mean(values, axis=-1, keepdims=True)
    centered = values - average
    variance = jnp.mean(centered * centered, axis=-1, keepdims=True)
    inv_std = lax.rsqrt(variance + NORM_EPSILON)
    normed = centered * inv_std
    return (normed * gain_row + shift_row, normed, inv_std)


def norm_backward(upstream, normed, inv_std, gain_row):
    scaled = upstream * gain_row
    inner_mean = jnp.mean(scaled, axis=-1, keepdims=True)
    cross_mean = jnp.mean(scaled * normed, axis=-1, keepdims=True)
    return (
        inv_std * (scaled - inner_mean - normed * cross_mean),
        jnp.sum(upstream * normed, axis=0),
        jnp.sum(upstream, axis=0),
    )


def newton_schulz_rows(rows, width):
    total = rows.shape[0]
    count = total // width
    squares = jnp.sum(rows * rows, axis=1).reshape(count, width)
    frobenius = jnp.sqrt(jnp.sum(squares, axis=1))
    divisor = jnp.repeat(frobenius + 1e-07, width)[:, None]
    iterate = (rows / divisor).astype(jnp.bfloat16)
    unit_of = jnp.arange(total) // width
    same_unit = unit_of[:, None] == unit_of[None, :]
    for _ in range(NS_STEPS):
        gram = jnp.einsum("kd,ld->kl", iterate, iterate, preferred_element_type=jnp.float32)
        if count > 1:
            gram = jnp.where(same_unit, gram, 0.0)
        gram_matrix = gram.astype(jnp.bfloat16)
        square = jnp.dot(gram_matrix, gram_matrix, preferred_element_type=jnp.float32)
        polynomial = (
            SCHULZ_SECOND * gram_matrix.astype(jnp.float32) + SCHULZ_THIRD * square
        ).astype(jnp.bfloat16)
        iterate = (
            SCHULZ_FIRST * iterate.astype(jnp.float32)
            + jnp.dot(polynomial, iterate, preferred_element_type=jnp.float32)
        ).astype(jnp.bfloat16)
    return iterate


def vector_step(weight, momentum, gradient):
    new_momentum = MOMENTUM_BETA * momentum + gradient
    blocks = new_momentum.reshape(-1, HD)
    scaled = blocks * lax.rsqrt(jnp.mean(blocks * blocks, axis=-1, keepdims=True) + 1e-06)
    return (weight - VECTOR_RATE * scaled.reshape(weight.shape), new_momentum)


def pad_to(values, size, axis):
    missing = size - values.shape[axis]
    if missing == 0:
        return values
    pads = [(0, missing if at == axis else 0) for at in range(values.ndim)]
    return jnp.pad(values, pads)


def to_owners(shares, owned_width, dp_count):
    padded = pad_to(shares, owned_width * dp_count, 1)
    return padded.reshape(shares.shape[0], dp_count, owned_width).transpose(1, 0, 2)


def from_owners(parts, width):
    owners, share, owned_width = parts.shape
    return parts.transpose(1, 0, 2).reshape(share, owners * owned_width)[:, :width]


def exchange(parts):
    return lax.all_to_all(parts, "dp", 0, 0, tiled=True)


def swap(values):
    return lax.ppermute(values, "tensor", [(0, 1), (1, 0)])


def row_parts(values, paired):
    if paired:
        return [values, swap(values)]
    return [lax.all_gather(values, "tensor", axis=0, tiled=True)]


def joined_rows(parts):
    return parts[0] if len(parts) == 1 else jnp.concatenate(parts, axis=0)


def collect_product(parts, product):
    if len(parts) == 2:
        leaving = product(parts[1]).astype(jnp.bfloat16)
        return product(parts[0]) + swap(leaving).astype(jnp.float32)
    return lax.psum_scatter(
        product(parts[0]).astype(jnp.bfloat16), "tensor", scatter_dimension=0, tiled=True
    ).astype(jnp.float32)


TILE = 256
SPAN = 512
REACH = -(-(SPAN - 1) // TILE)
MASKED = 1e30


def tile_pairs(length):
    return [
        (at_query, at_key)
        for at_query in range(length // TILE)
        for at_key in range(max(0, at_query - REACH), at_query + 1)
    ]


def contract(left, right, dims):
    return lax.dot_general(left, right, (dims, ((), ())), preferred_element_type=jnp.float32)


def fill_distance(row_seg, col_seg, distance, pairs):
    for slot, (at_query, at_key) in enumerate(pairs):
        query_seg = row_seg[0, :, at_query * TILE : (at_query + 1) * TILE]
        key_seg = col_seg[0, at_key * TILE : (at_key + 1) * TILE, :]
        gap = (
            lax.broadcasted_iota(jnp.int32, (TILE, TILE), 1)
            - lax.broadcasted_iota(jnp.int32, (TILE, TILE), 0)
            + (at_query - at_key) * TILE
        )
        allowed = (key_seg == query_seg) & (gap >= 0)
        distance[slot] = jnp.where(allowed, gap.astype(jnp.float32), MASKED)


def tile_rows(first_row, length, index):
    row = index * TILE - first_row
    row = jnp.where(row < 0, row + length, row)
    return pl.ds(pl.multiple_of(row, TILE), TILE)


def attention_kernel(first_row, slopes, row_seg, col_seg, joined, out, inverse, distance):
    length = joined.shape[0]
    pairs = tile_pairs(length)
    duo = pl.program_id(1)

    @pl.when(duo == 0)
    def _():
        fill_distance(row_seg, col_seg, distance, pairs)

    for at_query in range(length // TILE):
        query_rows = tile_rows(first_row[0], length, at_query)
        pieces = []
        for part in range(2):
            slope = slopes[2 * duo + part]
            col = 3 * HD * part
            query = joined[query_rows, col : col + HD] * jnp.bfloat16(HD ** (-0.5))
            total = jnp.zeros((1, TILE), jnp.float32)
            gathered = jnp.zeros((HD, TILE), jnp.float32)
            for slot, (own, at_key) in enumerate(pairs):
                if own != at_query:
                    continue
                key_rows = tile_rows(first_row[0], length, at_key)
                key = joined[key_rows, col + HD : col + 2 * HD]
                value = joined[key_rows, col + 2 * HD : col + 3 * HD]
                weight = jnp.exp(contract(key, query, ((1,), (1,))) - slope * distance[slot])
                total = total + jnp.sum(weight, axis=0, keepdims=True)
                gathered = gathered + contract(
                    value, weight.astype(jnp.bfloat16), ((0,), (0,))
                )
            scale = 1.0 / total
            inverse[0, 0, part : part + 1, at_query * TILE : (at_query + 1) * TILE] = scale
            pieces.append(gathered * scale)
        out[query_rows, :] = jnp.concatenate(pieces, axis=0).T.astype(jnp.bfloat16)


def attention_grad_kernel(
    first_row,
    slopes,
    row_seg,
    col_seg,
    joined,
    attended,
    grads,
    inverse,
    out,
    sums,
    distance,
    delta,
    query_total,
):
    length = joined.shape[0]
    pairs = tile_pairs(length)
    tiles = length // TILE
    duo = pl.program_id(1)

    @pl.when(duo == 0)
    def _():
        fill_distance(row_seg, col_seg, distance, pairs)

    for at in range(tiles):
        rows = tile_rows(first_row[0], length, at)
        both = (grads[rows, :].astype(jnp.float32) * attended[rows, :].astype(jnp.float32)).T
        for part in range(2):
            delta[part : part + 1, at * TILE : (at + 1) * TILE] = jnp.sum(
                both[part * HD : (part + 1) * HD], axis=0, keepdims=True
            )
    for part in range(2):
        slope = slopes[2 * duo + part]
        col = 3 * HD * part
        value_sum = jnp.zeros((1, HD), jnp.float32)
        query_sum = jnp.zeros((1, HD), jnp.float32)
        for at_key in range(tiles):
            key_rows = tile_rows(first_row[0], length, at_key)
            key = joined[key_rows, col + HD : col + 2 * HD]
            value = joined[key_rows, col + 2 * HD : col + 3 * HD]
            grad_key = jnp.zeros((TILE, HD), jnp.float32)
            grad_value = jnp.zeros((TILE, HD), jnp.float32)
            for slot, (at_query, own) in enumerate(pairs):
                if own != at_key:
                    continue
                cols = slice(at_query * TILE, (at_query + 1) * TILE)
                query_rows = tile_rows(first_row[0], length, at_query)
                query = joined[query_rows, col : col + HD] * jnp.bfloat16(HD ** (-0.5))
                grad = grads[query_rows, part * HD : (part + 1) * HD]
                prob = (
                    jnp.exp(contract(key, query, ((1,), (1,))) - slope * distance[slot])
                    * inverse[0, 0, part : part + 1, cols]
                )
                d_prob = contract(value, grad, ((1,), (1,)))
                d_score = (prob * (d_prob - delta[part : part + 1, cols])).astype(jnp.bfloat16)
                grad_value = grad_value + contract(prob.astype(jnp.bfloat16), grad, ((1,), (0,)))
                grad_key = grad_key + contract(d_score, query, ((1,), (0,)))
                piece = contract(key, d_score, ((0,), (0,)))
                if at_key == max(0, at_query - REACH):
                    query_total[:, cols] = piece
                else:
                    query_total[:, cols] += piece
            out[key_rows, col + HD : col + 2 * HD] = grad_key.astype(jnp.bfloat16)
            out[key_rows, col + 2 * HD : col + 3 * HD] = grad_value.astype(jnp.bfloat16)
            value_sum = value_sum + jnp.sum(grad_value, axis=0, keepdims=True)
        for at_query in range(tiles):
            grad_query = query_total[:, at_query * TILE : (at_query + 1) * TILE].T * HD ** (-0.5)
            out[tile_rows(first_row[0], length, at_query), col : col + HD] = grad_query.astype(
                jnp.bfloat16
            )
            query_sum = query_sum + jnp.sum(grad_query, axis=0, keepdims=True)
        sums[0, 0, :, part * 2 * HD : part * 2 * HD + HD] = query_sum
        sums[0, 0, :, part * 2 * HD + HD : (part + 1) * 2 * HD] = value_sum


def attention_specs(length):
    whole = pl.BlockSpec(memory_space=pltpu.SMEM)
    return [
        whole,
        whole,
        pl.BlockSpec((1, 1, length), lambda s, m: (s, 0, 0)),
        pl.BlockSpec((1, length, 1), lambda s, m: (s, 0, 0)),
        pl.BlockSpec((length, 6 * HD), lambda s, m: (s, m)),
    ]


def attention(first_row, slopes, segments, joined):
    seq_count, length = segments.shape
    duos = joined.shape[1] // (6 * HD)
    work = seq_count * duos * 2 * len(tile_pairs(length)) * TILE * TILE
    return pl.pallas_call(
        attention_kernel,
        grid=(seq_count, duos),
        in_specs=attention_specs(length),
        out_specs=[
            pl.BlockSpec((length, 2 * HD), lambda s, m: (s, m)),
            pl.BlockSpec((1, 1, 2, length), lambda s, m: (s, m, 0, 0)),
        ],
        out_shape=[
            jax.ShapeDtypeStruct((seq_count * length, 2 * HD * duos), jnp.bfloat16),
            jax.ShapeDtypeStruct((seq_count, duos, 2, length), jnp.float32),
        ],
        scratch_shapes=[pltpu.VMEM((len(tile_pairs(length)), TILE, TILE), jnp.float32)],
        cost_estimate=pl.CostEstimate(
            flops=4 * work * HD, transcendentals=work, bytes_accessed=10 * joined.size // 3
        ),
        name="attention",
    )(first_row, slopes, segments[:, None, :], segments[:, :, None], joined)


def attention_grad(first_row, slopes, segments, joined, attended, grads, inverse):
    seq_count, length = segments.shape
    duos = joined.shape[1] // (6 * HD)
    work = seq_count * duos * 2 * len(tile_pairs(length)) * TILE * TILE
    return pl.pallas_call(
        attention_grad_kernel,
        grid=(seq_count, duos),
        in_specs=attention_specs(length)
        + [
            pl.BlockSpec((length, 2 * HD), lambda s, m: (s, m)),
            pl.BlockSpec((length, 2 * HD), lambda s, m: (s, m)),
            pl.BlockSpec((1, 1, 2, length), lambda s, m: (s, m, 0, 0)),
        ],
        out_specs=[
            pl.BlockSpec((length, 6 * HD), lambda s, m: (s, m)),
            pl.BlockSpec((1, 1, 1, 4 * HD), lambda s, m: (s, m, 0, 0)),
        ],
        out_shape=[
            jax.ShapeDtypeStruct(joined.shape, jnp.bfloat16),
            jax.ShapeDtypeStruct((seq_count, duos, 1, 4 * HD), jnp.float32),
        ],
        scratch_shapes=[
            pltpu.VMEM((len(tile_pairs(length)), TILE, TILE), jnp.float32),
            pltpu.VMEM((2, length), jnp.float32),
            pltpu.VMEM((HD, length), jnp.float32),
        ],
        cost_estimate=pl.CostEstimate(
            flops=10 * work * HD, transcendentals=work, bytes_accessed=16 * joined.size // 3
        ),
        name="attention_grad",
    )(first_row, slopes, segments[:, None, :], segments[:, :, None], joined, attended, grads, inverse)


def weight_grad_kernel(*refs):
    parts = (len(refs) - 1) // 2
    total = contract(refs[0][...], refs[parts][...], ((0,), (0,)))
    for at in range(1, parts):
        total = total + contract(refs[at][...], refs[parts + at][...], ((0,), (0,)))
    refs[-1][...] = total.astype(jnp.bfloat16)


def weight_grad(left_parts, right_parts, total_rows, first_row, earlier=None):
    width, depth = left_parts[0].shape[1], right_parts[0].shape[1]
    block = 256
    first_block = first_row // block
    tokens = sum(part.shape[0] for part in left_parts)
    in_specs = [
        pl.BlockSpec((part.shape[0], block), lambda i: (0, i)) for part in left_parts
    ] + [pl.BlockSpec(part.shape, lambda i: (0, 0)) for part in right_parts]
    args = [*left_parts, *right_parts]
    aliases = {}
    body = weight_grad_kernel
    if earlier is not None:
        in_specs.append(pl.BlockSpec(memory_space=pl.ANY))
        aliases = {len(args): 0}
        args.append(earlier)

        def body(*refs):
            weight_grad_kernel(*refs[:-2], refs[-1])

    return pl.pallas_call(
        body,
        grid=(width // block,),
        in_specs=in_specs,
        out_specs=pl.BlockSpec((block, depth), lambda i: (first_block + i, 0)),
        out_shape=jax.ShapeDtypeStruct((total_rows, depth), jnp.bfloat16),
        input_output_aliases=aliases,
        cost_estimate=pl.CostEstimate(
            flops=2 * tokens * width * depth,
            transcendentals=0,
            bytes_accessed=2 * (tokens * (width + depth) + width * depth),
        ),
        name="weight_grad",
    )(*args)


def gather_kernel(depth, shard, out, z_send, z_recv, x_send, x_recv, c_send, c_recv, own_sem):
    me = lax.axis_index("dp")
    core, column, level = me % 2, (me // 2) % 2, me // 4
    share = shard.shape[0]

    def place(at_level, at_column, at_core):
        return (at_level * 2 + at_column) * 2 + at_core

    def rows(block):
        return out.at[pl.ds(pl.multiple_of(block * share, share), share), :]

    def send(source, block, sends, recvs, target):
        return pltpu.make_async_remote_copy(
            src_ref=source,
            dst_ref=rows(block),
            send_sem=sends,
            recv_sem=recvs,
            device_id={"dp": target},
            device_id_type=pl.DeviceIdType.MESH,
        )

    across, beside = place(level, 1 - column, core), place(level, column, 1 - core)
    barrier = pltpu.get_barrier_semaphore()
    for target in (across, beside):
        pl.semaphore_signal(
            barrier, inc=1, device_id={"dp": target}, device_id_type=pl.DeviceIdType.MESH
        )
    for way in (1, -1):
        @pl.when((level + way >= 0) & (level + way < depth))
        def _():
            pl.semaphore_signal(
                barrier,
                inc=1,
                device_id={"dp": place(level + way, column, core)},
                device_id_type=pl.DeviceIdType.MESH,
            )
    peers = 2 + (level + depth - 1) // depth + (2 * depth - 2 - level) // depth
    pl.semaphore_wait(barrier, peers)

    def along(side, way, hop):
        origin = level - way * hop
        block = place(origin, column, core)
        source = shard if hop == 0 else rows(block)
        return send(
            source,
            block,
            z_send.at[side, hop],
            z_recv.at[side, hop],
            place(level + way, column, core),
        )

    def over(slot, origin, first):
        block = place(origin, column, core)
        return send(
            shard if first else rows(block), block, x_send.at[slot], x_recv.at[slot], across
        )

    def down(slot, block, first):
        return send(shard if first else rows(block), block, c_send.at[slot], c_recv.at[slot], beside)

    sides = ((0, 1), (1, -1))
    span = depth - 1

    def slot_of(side, hop):
        return 1 + side * span + hop - 1

    for side, way in sides:
        @pl.when((level + way >= 0) & (level + way < depth))
        def _():
            along(side, way, 0).start()
    over(0, level, True).start()
    down(0, me, True).start()
    own = pltpu.make_async_copy(shard, rows(me), own_sem)
    own.start()
    total = 2 * span + 1

    def arrived(slot, origin):
        over(slot, origin, False).wait_recv()
        down(total + slot, place(origin, 1 - column, core), False).start()

    for hop in range(1, depth):
        for side, way in sides:
            @pl.when((level - way * hop >= 0) & (level - way * hop < depth))
            def _():
                along(side, way, hop - 1).wait_recv()

                @pl.when((level + way >= 0) & (level + way < depth))
                def _():
                    along(side, way, hop).start()

                origin = level - way * hop
                over(slot_of(side, hop), origin, False).start()
                down(slot_of(side, hop), place(origin, column, core), False).start()

        if hop == 1:
            arrived(0, level)
        else:
            for side, way in sides:
                @pl.when((level - way * (hop - 1) >= 0) & (level - way * (hop - 1) < depth))
                def _():
                    arrived(slot_of(side, hop - 1), level - way * (hop - 1))

    for side, way in sides:
        @pl.when((level - way * span >= 0) & (level - way * span < depth))
        def _():
            arrived(slot_of(side, span), level - way * span)

    own.wait()
    over(0, level, True).wait_send()
    for base in (0, total):
        down(base, me, True).wait()
    for side, way in sides:
        @pl.when((level + way >= 0) & (level + way < depth))
        def _():
            along(side, way, 0).wait_send()

        for hop in range(1, depth):
            @pl.when((level - way * hop >= 0) & (level - way * hop < depth))
            def _():
                slot = slot_of(side, hop)
                over(slot, level, False).wait_send()
                down(slot, me, False).wait()
                down(total + slot, me, False).wait()

                @pl.when((level + way >= 0) & (level + way < depth))
                def _():
                    along(side, way, hop).wait_send()


def gather_rows(shard, dp_count):
    share, width = shard.shape
    depth = dp_count // 4
    span = depth - 1
    dma = pltpu.SemaphoreType.DMA
    return pl.pallas_call(
        functools.partial(gather_kernel, depth),
        out_shape=jax.ShapeDtypeStruct((share * dp_count, width), shard.dtype),
        in_specs=[pl.BlockSpec(memory_space=pltpu.VMEM)],
        out_specs=pl.BlockSpec(memory_space=pltpu.VMEM),
        scratch_shapes=[
            dma((2, depth)),
            dma((2, depth)),
            dma((2 * span + 1,)),
            dma((2 * span + 1,)),
            dma((4 * span + 2,)),
            dma((4 * span + 2,)),
            dma,
        ],
        compiler_params=pltpu.CompilerParams(collective_id=0, has_side_effects=True),
        cost_estimate=pl.CostEstimate(
            flops=0, transcendentals=0, bytes_accessed=32 * share * dp_count * width
        ),
        name="gather_rows",
    )(shard)


def local(
    hidden_in,
    out_cotangent,
    segment_ids,
    joined_weight,
    dense_weight,
    upward_weight,
    downward_weight,
    head_bias,
    upward_bias,
    norm_gain,
    row_bias,
    joined_momentum,
    dense_momentum,
    upward_momentum,
    downward_momentum,
    head_bias_momentum,
    upward_bias_momentum,
    norm_gain_momentum,
    row_bias_momentum,
):
    tensor_pos = lax.axis_index("tensor")
    dp_count = lax.axis_size("dp")
    share = joined_weight.shape[0]
    joined_width = joined_weight.shape[1]
    head_width = dense_weight.shape[0]
    hidden_width = upward_weight.shape[1]
    head_count = head_width // HD
    seq_count, _ = segment_ids.shape
    own_rows = hidden_in.shape[0]
    paired = lax.axis_size("tensor") == 2 and seq_count == 1
    attn_width = joined_width + head_width
    feed_width = 2 * hidden_width
    attn_owned = -(-(attn_width // HD) // dp_count) * HD
    feed_owned = -(-(feed_width // MB) // dp_count) * MB

    residual = hidden_in.astype(jnp.float32)
    first_out, first_normed, first_inv = layer_norm(residual, norm_gain[0], row_bias[0])
    first_all = joined_rows(row_parts(first_out.astype(jnp.bfloat16), paired))
    attn_share = jnp.concatenate([joined_weight, dense_weight.T], axis=1).astype(jnp.bfloat16)
    feed_share = jnp.concatenate([upward_weight, downward_weight.T], axis=1).astype(jnp.bfloat16)
    if paired and dp_count == 16:
        attn_share, feed_share = lax.optimization_barrier((attn_share, feed_share))
        attn_low = gather_rows(attn_share, dp_count)
    else:
        attn_low = lax.all_gather(attn_share, "dp", axis=0, tiled=True)
    feed_low = lax.all_gather(feed_share, "dp", axis=0, tiled=True)
    joined_low = attn_low[:, :joined_width]
    dense_low = attn_low[:, joined_width:]
    upward_low = feed_low[:, :hidden_width]
    downward_low = feed_low[:, hidden_width:]
    upstream = out_cotangent.astype(jnp.float32)
    upstream_parts = row_parts(out_cotangent, paired)
    first_all, upstream_parts = lax.optimization_barrier((first_all, upstream_parts))
    old_owned = exchange(
        jnp.concatenate(
            [
                to_owners(
                    jnp.concatenate([joined_momentum, dense_momentum.T], axis=1).astype(
                        jnp.bfloat16
                    ),
                    attn_owned,
                    dp_count,
                ),
                to_owners(
                    jnp.concatenate([upward_momentum, downward_momentum.T], axis=1).astype(
                        jnp.bfloat16
                    ),
                    feed_owned,
                    dp_count,
                ),
            ],
            axis=2,
        ).reshape(D, attn_owned + feed_owned)
    )

    slopes = jnp.exp2(
        -8.0 * (tensor_pos * head_count + jnp.arange(head_count) + 1).astype(jnp.float32) / H
    )
    no_bias = jnp.zeros((head_count, HD), jnp.float32)
    joined_bias = jnp.stack(
        [head_bias[0].reshape(head_count, HD), no_bias, head_bias[1].reshape(head_count, HD)],
        axis=1,
    ).reshape(joined_width)
    joined_all = (
        jnp.dot(first_all, joined_low, preferred_element_type=jnp.float32) + joined_bias
    ).astype(jnp.bfloat16)
    first_row = (tensor_pos * own_rows if paired else 0 * tensor_pos).astype(jnp.int32).reshape(1)
    attended_flat, inverse_totals = attention(first_row, slopes, segment_ids, joined_all)
    attended_parts = (
        [attended_flat[:own_rows], attended_flat[own_rows:]] if paired else [attended_flat]
    )
    attn_out = collect_product(
        attended_parts,
        lambda rows: jnp.einsum("tk,dk->td", rows, dense_low, preferred_element_type=jnp.float32),
    )
    middle = residual + attn_out + row_bias[1]
    second_out, second_normed, second_inv = layer_norm(middle, norm_gain[1], row_bias[2])
    second_parts = row_parts(second_out.astype(jnp.bfloat16), paired)
    pre_parts = [
        jnp.dot(rows, upward_low, preferred_element_type=jnp.float32) + upward_bias
        for rows in second_parts
    ]
    act_parts = [gelu_value(rows).astype(jnp.bfloat16) for rows in pre_parts]
    d_pre_parts = []
    for cot, pre in zip(upstream_parts, pre_parts):
        d_pre_parts.append(
            jnp.dot(cot, downward_low, preferred_element_type=jnp.float32) * gelu_slope(pre)
        )
    upbias_parts = [jnp.sum(rows, axis=0) for rows in d_pre_parts]
    upbias_local = sum(lax.optimization_barrier(upbias_parts))
    d_pre_low = [rows.astype(jnp.bfloat16) for rows in d_pre_parts]
    d_second = collect_product(
        d_pre_low,
        lambda rows: jnp.einsum("tf,df->td", rows, upward_low, preferred_element_type=jnp.float32),
    )
    feed_rows = feed_owned * dp_count
    if feed_rows == feed_width:
        feed_local = weight_grad(act_parts, upstream_parts, feed_rows, hidden_width)
        feed_local = weight_grad(d_pre_low, second_parts, feed_rows, 0, feed_local)
    else:
        upward_local = weight_grad(d_pre_low, second_parts, hidden_width, 0)
        downward_local = weight_grad(act_parts, upstream_parts, hidden_width, 0)
        feed_local = pad_to(
            jnp.concatenate([upward_local, downward_local], axis=0), feed_rows, 0
        )
    d_middle_norm, gain_second, shift_second = norm_backward(
        d_second, second_normed, second_inv, norm_gain[1]
    )
    d_middle = upstream + d_middle_norm
    d_middle, middle_later, act_later = lax.optimization_barrier((d_middle, middle, act_parts))
    mlp_out = collect_product(
        act_later,
        lambda rows: jnp.einsum(
            "tf,df->td", rows, downward_low, preferred_element_type=jnp.float32
        ),
    )
    block_out = (middle_later + mlp_out + row_bias[3]).astype(jnp.bfloat16)
    d_middle_all = joined_rows(row_parts(d_middle.astype(jnp.bfloat16), paired))
    d_attended = jnp.dot(d_middle_all, dense_low, preferred_element_type=jnp.float32).astype(
        jnp.bfloat16
    )
    feed_grad = lax.psum_scatter(feed_local, "dp", scatter_dimension=0, tiled=True)
    d_joined, head_sums = attention_grad(
        first_row, slopes, segment_ids, joined_all, attended_flat, d_attended, inverse_totals
    )
    head_sums = jnp.sum(head_sums, axis=0).reshape(head_count, 2, HD)
    head_local = head_sums.transpose(1, 0, 2).reshape(2, head_width)
    attn_rows = attn_owned * dp_count
    if attn_rows == attn_width and joined_width % 256 == 0 and head_width % 256 == 0:
        attn_local = weight_grad([attended_flat], [d_middle_all], attn_rows, joined_width)
        attn_local = weight_grad([d_joined], [first_all], attn_rows, 0, attn_local)
    else:
        joined_local = jnp.einsum(
            "tc,td->cd", d_joined, first_all, preferred_element_type=jnp.float32
        ).astype(jnp.bfloat16)
        dense_local = jnp.einsum(
            "tk,td->kd", attended_flat, d_middle_all, preferred_element_type=jnp.float32
        ).astype(jnp.bfloat16)
        attn_local = pad_to(jnp.concatenate([joined_local, dense_local], axis=0), attn_rows, 0)
    attn_grad = lax.psum_scatter(attn_local, "dp", scatter_dimension=0, tiled=True)
    d_joined_parts = [d_joined[:own_rows], d_joined[own_rows:]] if paired else [d_joined]
    d_first = collect_product(
        d_joined_parts,
        lambda rows: jnp.einsum("tc,dc->td", rows, joined_low, preferred_element_type=jnp.float32),
    )
    d_input_norm, gain_first, shift_first = norm_backward(
        d_first, first_normed, first_inv, norm_gain[0]
    )
    input_grad = d_middle + d_input_norm
    gain_local = jnp.stack([gain_first, gain_second])
    shift_local = jnp.stack(
        [shift_first, jnp.sum(d_middle, axis=0), shift_second, jnp.sum(upstream, axis=0)]
    )
    head_full = lax.dynamic_update_slice_in_dim(
        jnp.zeros((2, D), jnp.float32), head_local, tensor_pos * head_width, 1
    )
    upbias_full = lax.dynamic_update_slice_in_dim(
        jnp.zeros((FF,), jnp.float32), upbias_local, tensor_pos * hidden_width, 0
    )
    vector_total = lax.psum(
        jnp.concatenate([gain_local, shift_local, head_full, upbias_full.reshape(FF // D, D)]),
        ("dp", "tensor"),
    )
    norm_gain_grad, row_bias_grad = vector_total[:2], vector_total[2:6]
    head_bias_grad = lax.dynamic_slice_in_dim(
        vector_total[6:8], tensor_pos * head_width, head_width, 1
    )
    upward_bias_grad = lax.dynamic_slice_in_dim(
        vector_total[8:].reshape(FF), tensor_pos * hidden_width, hidden_width, 0
    )

    def owner_step(grad_rows, old_columns, width):
        momentum_rows = MOMENTUM_BETA * old_columns.T.astype(jnp.float32) + grad_rows.astype(
            jnp.float32
        )
        orthogonal = newton_schulz_rows(momentum_rows, width)
        owned = grad_rows.shape[0]
        both = jnp.concatenate([grad_rows, orthogonal], axis=0).T.reshape(
            dp_count, share, 2 * owned
        )
        back = exchange(both.reshape(dp_count * share, 2 * owned)).reshape(
            dp_count, share, 2 * owned
        )
        return (back[:, :, :owned], back[:, :, owned:])

    feed_back, feed_ortho = owner_step(feed_grad, old_owned[:, attn_owned:], MB)
    attn_back, attn_ortho = owner_step(attn_grad, old_owned[:, :attn_owned], HD)
    feed_back, feed_ortho = (
        from_owners(rows, feed_width).astype(jnp.float32) for rows in (feed_back, feed_ortho)
    )
    attn_back, attn_ortho = (
        from_owners(rows, attn_width).astype(jnp.float32) for rows in (attn_back, attn_ortho)
    )
    joined_grad, dense_grad = attn_back[:, :joined_width], attn_back[:, joined_width:].T
    upward_grad, downward_grad = feed_back[:, :hidden_width], feed_back[:, hidden_width:].T
    joined_ortho, dense_ortho = attn_ortho[:, :joined_width], attn_ortho[:, joined_width:].T
    upward_ortho, downward_ortho = feed_ortho[:, :hidden_width], feed_ortho[:, hidden_width:].T
    joined_mom_new = MOMENTUM_BETA * joined_momentum + joined_grad
    dense_mom_new = MOMENTUM_BETA * dense_momentum + dense_grad
    upward_mom_new = MOMENTUM_BETA * upward_momentum + upward_grad
    downward_mom_new = MOMENTUM_BETA * downward_momentum + downward_grad
    muon_step = MUON_RATE * 0.2 * math.sqrt(D)
    joined_new = joined_weight - muon_step * joined_ortho
    dense_new = dense_weight - muon_step * dense_ortho
    upward_new = upward_weight - muon_step * upward_ortho
    downward_new = downward_weight - muon_step * downward_ortho
    head_new, head_mom_new = vector_step(head_bias, head_bias_momentum, head_bias_grad)
    upbias_new, upbias_mom_new = vector_step(upward_bias, upward_bias_momentum, upward_bias_grad)
    gain_new, gain_mom_new = vector_step(norm_gain, norm_gain_momentum, norm_gain_grad)
    shift_new, shift_mom_new = vector_step(row_bias, row_bias_momentum, row_bias_grad)
    return (
        block_out,
        input_grad,
        joined_grad,
        dense_grad,
        upward_grad,
        downward_grad,
        head_bias_grad,
        upward_bias_grad,
        norm_gain_grad,
        row_bias_grad,
        joined_new,
        dense_new,
        upward_new,
        downward_new,
        head_new,
        upbias_new,
        gain_new,
        shift_new,
        joined_mom_new,
        dense_mom_new,
        upward_mom_new,
        downward_mom_new,
        head_mom_new,
        upbias_mom_new,
        gain_mom_new,
        shift_mom_new,
    )


def solution(mesh):
    return jax.shard_map(
        local,
        mesh=mesh,
        in_specs=(
            P(("dp", "tensor"), None),
            P(("dp", "tensor"), None),
            P("dp", None),
            P("dp", "tensor"),
            P("tensor", "dp"),
            P("dp", "tensor"),
            P("tensor", "dp"),
            P(None, "tensor"),
            P("tensor"),
            P(),
            P(),
            P("dp", "tensor"),
            P("tensor", "dp"),
            P("dp", "tensor"),
            P("tensor", "dp"),
            P(None, "tensor"),
            P("tensor"),
            P(),
            P(),
        ),
        out_specs=(
            P(("dp", "tensor"), None),
            P(("dp", "tensor"), None),
            P("dp", "tensor"),
            P("tensor", "dp"),
            P("dp", "tensor"),
            P("tensor", "dp"),
            P(None, "tensor"),
            P("tensor"),
            P(),
            P(),
            P("dp", "tensor"),
            P("tensor", "dp"),
            P("dp", "tensor"),
            P("tensor", "dp"),
            P(None, "tensor"),
            P("tensor"),
            P(),
            P(),
            P("dp", "tensor"),
            P("tensor", "dp"),
            P("dp", "tensor"),
            P("tensor", "dp"),
            P(None, "tensor"),
            P("tensor"),
            P(),
            P(),
        ),
        check_vma=False,
    )
```
